256 devices in a mesh: query: 4 (over x), corpus: 64 (over y, z, core).
Axes of the slice: x: 4, y: 4, z: 8, core: 2. Of those that a mesh axis runs over, the one named last changes fastest.
Arguments:
- queries: float32 [256, 32, 128], P(('query', 'corpus')), may hold values from -6 to 6
- passages: float32 [1024, 180, 128], P(('query', 'corpus')), may hold values from -0.5 to 0.5
- clusters: int32 [1024, 180], P(('query', 'corpus')), may hold values from 0 to 23
- lengths: int32 [1024], P(('query', 'corpus')), may hold values from 45 to 180, as said below
- feedback: int32 [256, 3], replicated, may hold values from 0 to 1023, as said below
- ranks: int32 [256, 24], replicated, may hold values from 0 to 23, each once within a row
- cand_local: int32 [256, 512], P(None, ('query', 'corpus')), may hold values from 0 to 3
- cand_count: int32 [256, 256], P(None, ('query', 'corpus')), may hold values from 1 to 2, as said below
Outputs:
- scores: float32 [256, 512], P(('query', 'corpus'))
The draws below stay inside these ranges and needn't reach their ends.
Inputs may be any that keep to these rules, and one draw needn't show every extreme that they name: `lengths`: some passages fill all 180 slots of their tile. `cand_count`: each query fills all 2 slots on at least one device. The passages of exactly 3 of the (query, feedback) pairs lie on each device. `ranks`: each row is a permutation of 0 to 23.
All inputs are finite; a program needn't handle non-finite values.
Results may differ from the reference program's by a relative error of at most 0.0003.
Values sent between devices are 32-bit elements; how exact they have to be, the bound alone decides.
A program may use at most 64 MiB of HBM per device.

```python
import jax
import jax.numpy as jnp
from jax import lax

DIM = 128
QL = 32
PL = 180
FB = 3
NCENT = 24
EXP = 10
CAP = 2
Q_DEV = 1
P_DEV = 4
QUERIES = 256
PASSAGES = 1024
SLOTS = 512
DEVICES = 256


def draw_lengths(key, part):
    first, second = jax.random.split(key)
    common = jax.random.randint(first, (PASSAGES,), PL // 4, PL + 1)
    offset = jax.random.randint(second, (), 0, 16)
    filled = jnp.arange(PASSAGES) % 16 == offset
    return jnp.where(filled, PL, common).astype(jnp.int32)


def draw_cand_count(key, part):
    first, second = jax.random.split(key)
    common = jax.random.randint(first, (QUERIES, DEVICES), 1, CAP + 1)
    chosen = jax.random.randint(second, (QUERIES, 1), 0, DEVICES)
    filled = jnp.arange(DEVICES)[None, :] == chosen
    return jnp.where(filled, CAP, common).astype(jnp.int32)


def draw_feedback(key, part):
    first, second = jax.random.split(jax.random.fold_in(key, 7))
    pairs = QUERIES * FB
    order = jax.random.permutation(first, pairs)
    device_of = order // (Q_DEV * FB)
    local = jax.random.randint(second, (pairs,), 0, P_DEV)
    return (device_of * P_DEV + local).reshape(QUERIES, FB).astype(jnp.int32)


def touch_ends(array, rng, least, high):
    dims = array.shape
    index_at = [jax.random.randint(jax.random.fold_in(rng, axis), (), 0, dims[axis]) for axis in range(len(dims))]
    array = array.at[tuple(index_at)].set(least)
    longest = dims.index(max(dims))
    index_at[longest] = (index_at[longest] + 1) % dims[longest]
    return array.at[tuple(index_at)].set(high)


def levels(key, extent, cuts, low, largest):
    gain, own = 1.0, jax.random.fold_in(key, 6)
    for dim, parts in cuts:
        steps = jnp.exp(jax.random.uniform(jax.random.fold_in(own, dim), (parts,), jnp.float32, low / len(cuts), largest / len(cuts)))
        gain = gain * jnp.repeat(steps, extent[dim] // parts).reshape([-1 if axis == dim else 1 for axis in range(len(extent))])
    return gain


def centred(stream_key, shape, width, most, shards=(), held_as=jnp.bfloat16):
    values = jax.random.normal(stream_key, shape, jnp.float32) * width
    if len(shards) > 0:
        values = levels(stream_key, shape, shards, -0.22, 0.18) * values
    return jnp.clip(values, min=-most, max=most).astype(held_as)


def setup_inputs(seed: int = 0) -> dict:
    key_of = jax.random.split(jax.random.key(seed), 9)
    return {
        "queries": centred(key_of[0], (QUERIES, QL, DIM), 1.0, 6.0, ((0, 256),), jnp.float32),
        "passages": centred(key_of[1], (PASSAGES, PL, DIM), DIM ** -0.5, 0.5, ((0, 256),), jnp.float32),
        "clusters": touch_ends(jax.random.randint(key_of[2], (PASSAGES, PL), 0, NCENT), jax.random.fold_in(key_of[2], 1), 0, NCENT - 1).astype(jnp.int32),
        "lengths": draw_lengths(jax.random.fold_in(key_of[8], 71), 0),
        "feedback": draw_feedback(jax.random.fold_in(key_of[8], 71), 0),
        "ranks": jax.vmap(lambda own: jax.random.permutation(own, NCENT))(jax.random.split(key_of[5], QUERIES)).reshape((QUERIES, NCENT)).astype(jnp.int32),
        "cand_local": touch_ends(jax.random.randint(key_of[6], (QUERIES, SLOTS), 0, P_DEV), jax.random.fold_in(key_of[6], 1), 0, P_DEV - 1).astype(jnp.int32),
        "cand_count": draw_cand_count(jax.random.fold_in(key_of[8], 71), 0),
    }


beta_prf = 0.5
highest = lax.Precision.HIGHEST

def idf_weights():
    order = jnp.arange(EXP).astype(jnp.float32)
    return beta_prf * jnp.log((NCENT + 1.0) / (order + 1.0))

def expand_tokens(tokens, sums, ranking):
    scale = lax.rsqrt(lax.optimization_barrier(jnp.mean(sums * sums, axis=-1, keepdims=True)) + 1e-05)
    centroid = sums * scale
    select = (ranking[:, None, :] == jnp.arange(EXP, dtype=jnp.int32)[None, :, None]).astype(jnp.float32)
    extra = jnp.einsum('njk,nkd->njd', select, centroid, precision=highest)
    extra = extra * idf_weights()[None, :, None]
    return jnp.concatenate([tokens, extra], axis=1)

def maxsim(expanded, tiles, alive):
    similar = jnp.einsum('ed,spd->sep', expanded, tiles, precision=highest)
    similar = jnp.where(alive[:, None, :], similar, -1e+30)
    return lax.optimization_barrier(jnp.sum(lax.optimization_barrier(jnp.max(similar, axis=2)), axis=1)) / QL

def reference(queries, passages, clusters, lengths, feedback, ranks, cand_local, cand_count):
    token_axis = jnp.arange(PL, dtype=jnp.int32)
    centre_axis = jnp.arange(NCENT, dtype=jnp.int32)

    def feedback_sums(feed_row):
        tiles = passages[feed_row]
        alive = token_axis[None, :] < lengths[feed_row][:, None]
        member = ((clusters[feed_row][:, None, :] == centre_axis[None, :, None]) & alive[:, None, :]).astype(jnp.float32)
        return jnp.einsum('fkt,ftd->kd', member, tiles, precision=highest)
    sums = lax.map(feedback_sums, feedback)
    expanded = expand_tokens(queries, sums, ranks)
    slot_axis = jnp.arange(SLOTS, dtype=jnp.int32)
    owner = slot_axis // CAP

    def score_query(items):
        row_expanded, row_local, row_count = items
        global_ids = (owner * P_DEV + row_local).astype(jnp.int32)
        tiles = passages[global_ids]
        alive = token_axis[None, :] < lengths[global_ids][:, None]
        values = maxsim(row_expanded, tiles, alive)
        valid = slot_axis % CAP < row_count[owner]
        return jnp.where(valid, values, jnp.zeros_like(values))
    return lax.map(score_query, (expanded, cand_local, cand_count))
```

```python
import functools
import heapq
import math

import jax
import jax.numpy as jnp
from jax import lax
from jax.experimental import pallas as pl
from jax.experimental.pallas import tpu as pltpu
from jax.sharding import PartitionSpec as P

DIM = 128
QL = 32
PL = 180
NCENT = 24
EXP = 10
CAP = 2
FB = 3
NP = 4
NQ = 256
SIZE = {"x": 4, "y": 4, "z": 8}
CORES = 2
F32 = jnp.float32
BF16 = jnp.bfloat16
MESH = pl.DeviceIdType.MESH
WEIGHT = [0.5 * math.log((NCENT + 1.0) / (j + 1.0)) for j in range(EXP)]

PARTS = (
    ("q", 0, 8, "xyz"),
    ("q", 8, 8, "yzx"),
    ("q", 16, 16, "zxy"),
    ("i", 0, 8, "xyz"),
    ("i", 8, 16, "yzx"),
    ("i", 24, 8, "zxy"),
)
HOP_US = 1.8
LINK_GBS = 90.0
PAIR_US = 1.0
PAIR_GBS = 300.0
FINE = True


def ring(n, anti):
    half = n // 2
    return {
        1: [-k for k in range(1, half + (anti == 1))],
        -1: [k for k in range(1, half + (anti == -1))],
    }


def displacements(n):
    return [0] + [s * k for k in range(1, n // 2) for s in (-1, 1)] + [n // 2]


def split3(v):
    hi = v.astype(BF16)
    rest = v - hi.astype(F32)
    mid = rest.astype(BF16)
    low = (rest - mid.astype(F32)).astype(BF16)
    return hi, mid, low


class Gather:
    def __init__(self, bufs, recv_sem, send_sem, pair_recv, pair_send):
        self.bufs = bufs
        self.recv_sem, self.send_sem = recv_sem, send_sem
        self.pair_recv, self.pair_send = pair_recv, pair_send
        corpus = lax.axis_index("corpus")
        zc = SIZE["z"] * CORES
        self.me = {
            "x": lax.axis_index("query"),
            "y": corpus // zc,
            "z": (corpus // CORES) % SIZE["z"],
            "c": corpus % CORES,
        }
        self.heap = []
        self.count = 0
        self.n_recv = 0
        self.n_pair = 0
        self.link = {}
        self.now = 0.0
        self.state = {}

    def at(self, axis, d):
        if d == 0:
            return self.me[axis]
        n = SIZE[axis]
        return (self.me[axis] + (d % n)) & (n - 1)

    def device(self, **moved):
        pos = dict(self.me)
        pos.update(moved)
        return (pos["x"], (pos["y"] * SIZE["z"] + pos["z"]) * CORES + pos["c"])

    def region(self, part, sel, core):
        wave, row, rows, _ = PARTS[part]
        idx = []
        for axis in "xyz":
            d = sel[axis]
            idx.append(slice(None) if d is None else self.at(axis, d))
        return self.bufs[wave].at[idx[0], idx[1], idx[2], core, pl.ds(row, rows), :]

    def blocks(self, sel):
        return math.prod(SIZE[a] for a in "xyz" if sel[a] is None)

    def push(self, when, item):
        self.count += 1
        heapq.heappush(self.heap, (when, self.count, item))

    def send(self, part, stage, way, sel):
        axis = PARTS[part][3][stage]
        index = self.n_recv
        self.n_recv += 1
        ref = self.region(part, sel, self.me["c"])
        copy = pltpu.make_async_remote_copy(
            src_ref=ref,
            dst_ref=ref,
            send_sem=self.send_sem.at[part],
            recv_sem=self.recv_sem.at[index],
            device_id=self.device(**{axis: self.at(axis, way)}),
            device_id_type=MESH,
        )
        copy.start()
        bytes_ = self.blocks(sel) * PARTS[part][2] * DIM * 4
        key = (axis, way)
        begin = max(self.link.get(key, 0.0), self.now)
        self.link[key] = begin + 2 * bytes_ / (LINK_GBS * 1e3)
        self.now += 0.03
        got = dict(sel)
        got[axis] = sel[axis] - way
        self.push(self.link[key] + HOP_US, ("recv", part, stage, way, got, index))

    def pair(self, part, sel):
        index = self.n_pair
        self.n_pair += 1
        core = self.me["c"]
        ref = self.region(part, sel, core)
        copy = pltpu.make_async_remote_copy(
            src_ref=ref,
            dst_ref=ref,
            send_sem=self.pair_send.at[part],
            recv_sem=self.pair_recv.at[index],
            device_id=self.device(c=1 - core),
            device_id_type=MESH,
        )
        copy.start()
        bytes_ = self.blocks(sel) * PARTS[part][2] * DIM * 4
        begin = max(self.link.get("pair", 0.0), self.now)
        self.link["pair"] = begin + bytes_ / (PAIR_GBS * 1e3)
        self.now += 0.03
        self.push(self.link["pair"] + PAIR_US, ("pair", part, dict(sel), index))

    def ways(self, n, key, way, d):
        half = n // 2
        step = abs(d) + 1
        return step < half or (step == half and key == way)

    def start_stage(self, part, stage, sub, sel):
        n = SIZE[PARTS[part][3][stage]]
        anti = 1 if (sub + part) % 2 == 0 else -1
        for way in (1, -1):
            if self.ways(n, anti, way, 0):
                self.send(part, stage, way, sel)

    def begin(self, wave):
        for part, spec in enumerate(PARTS):
            if spec[0] != wave:
                continue
            a1, a2, a3 = spec[3]
            self.state[part] = {
                "line": set(), "plane": set(), "far": {}, "sub": {},
            }
            own = {"x": 0, "y": 0, "z": 0}
            self.start_stage(part, 0, 0, own)
        for part, spec in enumerate(PARTS):
            if spec[0] == wave:
                self.have1(part, 0)

    def have1(self, part, d1):
        a1, a2, a3 = PARTS[part][3]
        st = self.state[part]
        st["line"].add(d1)
        if FINE:
            sel = {a1: d1, a2: 0, a3: 0}
            sub = displacements(SIZE[a1]).index(d1)
            self.start_stage(part, 1, sub, sel)
        elif len(st["line"]) == SIZE[a1]:
            self.start_stage(part, 1, 0, {a1: None, a2: 0, a3: 0})
        if len(st["line"]) == SIZE[a1]:
            self.have2(part, 0)

    def got2(self, part, d2, sel):
        a1 = PARTS[part][3][0]
        st = self.state[part]
        if sel[a1] is None:
            self.have2(part, d2)
            return
        seen = st["sub"].setdefault(d2, set())
        seen.add(sel[a1])
        if len(seen) == SIZE[a1]:
            self.have2(part, d2)

    def have2(self, part, d2):
        a1, a2, a3 = PARTS[part][3]
        st = self.state[part]
        st["plane"].add(d2)
        sub = displacements(SIZE[a2]).index(d2)
        self.start_stage(part, 2, sub, {a1: None, a2: d2, a3: 0})
        if len(st["plane"]) == SIZE[a2]:
            self.pair(part, {a1: None, a2: None, a3: 0})

    def got3(self, part, d3, sel):
        a1, a2, a3 = PARTS[part][3]
        seen = self.state[part]["far"].setdefault(d3, set())
        seen.add(sel[a2])
        if len(seen) == SIZE[a2]:
            self.pair(part, {a1: None, a2: None, a3: d3})

    def canon(self, axis, d):
        n = SIZE[axis]
        return n // 2 if d is not None and abs(d) == n // 2 else d

    def handle(self, item):
        if item[0] == "pair":
            _, part, sel, index = item
            ref = self.region(part, sel, 1 - self.me["c"])
            pltpu.make_async_copy(ref, ref, self.pair_recv.at[index]).wait()
            return PARTS[part][0]
        _, part, stage, way, sel, index = item
        ref = self.region(part, sel, self.me["c"])
        pltpu.make_async_copy(ref, ref, self.recv_sem.at[index]).wait()
        order = PARTS[part][3]
        axis = order[stage]
        n = SIZE[axis]
        d = sel[axis]
        if stage == 0:
            sub = 0
        else:
            prev = order[stage - 1]
            sub = 0 if sel[prev] is None else displacements(SIZE[prev]).index(self.canon(prev, sel[prev]))
        anti = 1 if (sub + part) % 2 == 0 else -1
        if self.ways(n, anti, way, d):
            self.send(part, stage, way, sel)
        sel = dict(sel)
        sel[axis] = self.canon(axis, d)
        if stage == 0:
            self.have1(part, sel[axis])
        elif stage == 1:
            self.got2(part, sel[axis], sel)
        else:
            self.got3(part, sel[axis], sel)
        return None

    def run(self, tasks):
        left = {"q": 0, "i": 0}
        need = {"q": 0, "i": 0}
        for spec in PARTS:
            need[spec[0]] += SIZE[spec[3][2]]
        tasks = list(tasks)
        while self.heap:
            when, _, item = self.heap[0]
            while tasks and self.now + tasks[0][1] < when + 0.3 and left[tasks[0][0]] >= tasks[0][3]:
                task = tasks.pop(0)
                task[2]()
                self.now += task[1]
            heapq.heappop(self.heap)
            self.now = max(self.now, when)
            wave = self.handle(item)
            self.now += 0.01
            if wave:
                left[wave] += 1
        for task in tasks:
            task[2]()
            self.now += task[1]
        assert left == need

    def drain(self):
        for part, (wave, row, rows, _) in enumerate(PARTS):
            flat = self.bufs[wave].reshape(NQ, QL, DIM)
            ref = flat.at[pl.ds(0, NQ // 2 - 1), pl.ds(row, rows), :]
            pltpu.make_async_copy(ref, ref, self.send_sem.at[part]).wait()
            ref = flat.at[pl.ds(0, NQ // 2), pl.ds(row, rows), :]
            pltpu.make_async_copy(ref, ref, self.pair_send.at[part]).wait()


def iota(shape, axis):
    return lax.broadcasted_iota(jnp.int32, shape, axis)


def kernel(
    queries, rows_ref, clusters, lengths, feedback, ranks, cand, count, out,
    qbuf, ibuf, stage, p3, sel_ref, acc_ref,
    w_ref, r1_ref, m_ref, r2_ref,
    recv_sem, send_sem, pair_recv, pair_send, own_sem, a_send, a_recv, b_send, b_recv,
):
    gather = Gather({"q": qbuf, "i": ibuf}, recv_sem, send_sem, pair_recv, pair_send)
    me = gather.me
    home = lambda ref: ref.at[me["x"], me["y"], me["z"], me["c"]]

    own_q = pltpu.make_async_copy(queries.at[0], home(qbuf), own_sem.at[0])
    own_q.start()
    barrier = pltpu.get_barrier_semaphore()
    peers = [gather.device(**{a: gather.at(a, w)}) for a in "xyz" for w in (1, -1)]
    peers.append(gather.device(c=1 - me["c"]))
    for peer in peers:
        pl.semaphore_signal(barrier, inc=1, device_id=peer, device_id_type=MESH)
    pl.semaphore_wait(barrier, len(peers))
    own_q.wait()
    gather.begin("q")

    position = me["x"] * (NQ // 4) + (me["y"] * SIZE["z"] + me["z"]) * CORES + me["c"]
    fb = feedback[...]
    dev_row = (fb // NP).astype(F32)
    dev_col = jnp.transpose(jnp.concatenate([dev_row, jnp.zeros((8 - FB, NQ), F32)], axis=0))
    before = iota((NQ, NQ), 0) < iota((NQ, NQ), 1)
    turns = []
    for f in range(FB):
        total = jnp.zeros((NQ, NQ), F32)
        for g in range(FB):
            same = dev_col[:, g:g + 1] == dev_row[f:f + 1, :]
            if g == f:
                same = same & before
            if g <= f:
                total = total + jnp.where(same, 1.0, 0.0)
        turns.append(jnp.sum(total, axis=0, keepdims=True))
    turn_row = jnp.concatenate(turns, axis=0)

    rank_f = ranks[...].astype(F32)
    mine = dev_row == position.astype(F32)
    local_f = (fb % NP).astype(F32)
    columns, owners = [], []
    for i in range(FB):
        pick = jnp.where(mine & (turn_row == float(i)), 1.0, 0.0)
        owners.append(jnp.sum(jnp.sum(pick * local_f, axis=0, keepdims=True), axis=1, keepdims=True))
        who = jnp.sum(pick, axis=0, keepdims=True)
        columns.append(jnp.sum(rank_f * who, axis=1, keepdims=True))
    lane = iota((NCENT, QL), 1)
    turn = jnp.where(lane < EXP, 0, jnp.where(lane < 2 * EXP, 1, 2))
    place = (lane - turn * EXP).astype(F32)
    rank_of = jnp.where(turn == 0, columns[0], jnp.where(turn == 1, columns[1], columns[2]))
    owner_of = jnp.where(turn == 0, owners[0], jnp.where(turn == 1, owners[1], owners[2]))
    wanted = (rank_of == place) & (lane < FB * EXP)
    token = iota((NCENT, PL), 1)
    centre = iota((NCENT, PL), 0)
    asks, sums = [], []
    for p in range(NP):
        member = (clusters[p:p + 1, :] == centre) & (token < lengths[p])
        member = jnp.where(member, 1.0, 0.0).astype(BF16)
        tile = jnp.concatenate(split3(rows_ref[pl.ds(p, PL, stride=NP), :]), axis=1)
        part = jnp.dot(member, tile, preferred_element_type=F32)
        sums.append(part[:, :DIM] + part[:, DIM:2 * DIM] + part[:, 2 * DIM:])
        asks.append(jnp.where(wanted & (owner_of == float(p)), 1.0, 0.0))
    asks = jnp.transpose(jnp.concatenate(asks, axis=0)).astype(BF16)
    tile = jnp.concatenate(split3(jnp.concatenate(sums, axis=0)), axis=1)
    items = jnp.dot(asks, tile, preferred_element_type=F32)
    stage[...] = items[:, :DIM] + items[:, DIM:2 * DIM] + items[:, 2 * DIM:]

    turn_col = jnp.transpose(jnp.concatenate([turn_row, jnp.zeros((8 - FB, NQ), F32)], axis=0))
    device = iota((NQ, NQ), 1).astype(F32)
    for i in range(FB):
        total = jnp.zeros((NQ, NQ), F32)
        for f in range(FB):
            hit = (dev_col[:, f:f + 1] == device) & (turn_col[:, f:f + 1] == float(i))
            total = total + jnp.where(hit, 1.0, 0.0)
        sel_ref[:, i * NQ:(i + 1) * NQ] = total.astype(BF16)

    own_i = pltpu.make_async_copy(stage, home(ibuf), own_sem.at[1])
    own_i.start()

    live = rows_ref[...]
    row = iota((NP * PL, 1), 0)
    slot = row % NP
    length = jnp.where(slot == 0, lengths[0], jnp.where(slot == 1, lengths[1], jnp.where(slot == 2, lengths[2], lengths[3])))
    head = rows_ref[0:NP, :]
    head = jnp.concatenate([head, head] * (PL // 2), axis=0)
    live = jnp.where(row // NP < length, live, head)
    hi = live.astype(BF16)
    low = (live - hi.astype(F32)).astype(BF16)
    p3[:, 0:DIM] = hi
    p3[:, DIM:2 * DIM] = low
    p3[:, 2 * DIM:] = hi
    acc_ref[...] = jnp.zeros_like(acc_ref)

    own_i.wait()
    gather.now = 4.0
    gather.begin("i")

    def add_rows(tile):
        hi = tile.astype(BF16)
        low = (tile - hi.astype(F32)).astype(BF16)
        rhs = jnp.concatenate([hi, hi, low], axis=1)
        similar = lax.dot_general(p3[...], rhs, (((1,), (1,)), ((), ())), preferred_element_type=F32)
        best = jnp.max(similar.reshape(NP * PL // 8, 8, NQ), axis=0)
        acc_ref[...] += jnp.maximum(best, pltpu.roll(best, 4, 0))

    qflat = qbuf.reshape(NQ * QL, DIM)
    iflat = ibuf.reshape(NQ * QL, DIM)

    def score_queries(first, n):
        @pl.loop(first, first + n)
        def _(t):
            add_rows(qflat[pl.ds(t, NQ, stride=QL), :])

    need_q = sum(SIZE[s[3][2]] for s in PARTS if s[0] == "q")
    tasks = [("q", 0.5, functools.partial(score_queries, t, 1), need_q) for t in range(0, QL, 1)]
    gather.run(merge(tasks))

    @pl.loop(0, EXP)
    def _(j):
        pieces = [iflat[pl.ds(j + i * EXP, NQ, stride=QL), :] for i in range(FB)]
        tile = jnp.concatenate(pieces, axis=0)
        hi = tile.astype(BF16)
        low = (tile - hi.astype(F32)).astype(BF16)
        both = jnp.dot(sel_ref[...], jnp.concatenate([hi, low], axis=1), preferred_element_type=F32)
        total = both[:, :DIM] + both[:, DIM:]
        weight = jnp.float32(WEIGHT[EXP - 1])
        for k in range(EXP - 1):
            weight = jnp.where(j == k, jnp.float32(WEIGHT[k]), weight)
        scale = lax.rsqrt(jnp.mean(total * total, axis=1, keepdims=True) + 1e-05)
        add_rows(total * scale * weight)

    gather.drain()

    lines = SIZE["x"] * SIZE["y"]
    width = SIZE["z"] * CORES
    picked = cand[...]
    live_slots = count[...]
    w = jnp.zeros((lines, DIM), F32)
    own_row = iota((lines, NQ), 1) // width == iota((lines, NQ), 0)
    for s in range(CAP):
        value = jnp.zeros((1, NQ), F32)
        for p in range(NP):
            value = value + jnp.where(picked[s:s + 1, :] == p, acc_ref[p:p + 1, :], 0.0)
        value = jnp.where(live_slots > s, value * (1.0 / QL), 0.0)
        spread = jnp.where(own_row, value, 0.0)
        put = iota((NQ, DIM), 0) % width * CAP + s == iota((NQ, DIM), 1)
        put = jnp.where(put, 1.0, 0.0).astype(BF16)
        for term in split3(spread):
            w = w + jnp.dot(term, put, preferred_element_type=F32)
    for r in range(lines):
        w_ref[r] = w[r:r + 1, :]

    exchange(gather, w_ref, r1_ref, a_send, a_recv, "xy")
    r1 = jnp.concatenate([r1_ref[r] for r in range(lines)], axis=0)
    turned = jnp.transpose(r1)
    for r in range(width):
        m_ref[r, :, 0:lines] = turned[r * CAP:(r + 1) * CAP, :]
    exchange(gather, m_ref, r2_ref, b_send, b_recv, "zc")
    r2 = jnp.concatenate([r2_ref[r] for r in range(width)], axis=0)
    out[...] = jnp.transpose(r2)[0:lines, :]


def merge(tasks):
    return tasks


def exchange(gather, src, dst, send_sem, recv_sem, axes):
    me = gather.me
    sizes = {"x": SIZE["x"], "y": SIZE["y"], "z": SIZE["z"], "c": CORES}
    a, b = axes
    mine = me[a] * sizes[b] + me[b]
    steps = []
    for da in range(sizes[a]):
        for db in range(sizes[b]):
            if da or db:
                far = min(da, sizes[a] - da) + (min(db, sizes[b] - db) if b != "c" else 0.3 * db)
                steps.append((-far, da, db))
    steps.sort()
    copies = []
    for k, (_, da, db) in enumerate(steps):
        ta = (me[a] + da) & (sizes[a] - 1)
        tb = (me[b] + db) & (sizes[b] - 1)
        copy = pltpu.make_async_remote_copy(
            src_ref=src.at[ta * sizes[b] + tb],
            dst_ref=dst.at[mine],
            send_sem=send_sem.at[k],
            recv_sem=recv_sem.at[k],
            device_id=gather.device(**{a: ta, b: tb}),
            device_id_type=MESH,
        )
        copy.start()
        copies.append((copy, da, db))
    dst[mine] = src[mine]
    for k, (copy, da, db) in enumerate(copies):
        fa = (me[a] - da) & (sizes[a] - 1)
        fb = (me[b] - db) & (sizes[b] - 1)
        ref = dst.at[fa * sizes[b] + fb]
        pltpu.make_async_copy(ref, ref, recv_sem.at[k]).wait()
    for copy, _, _ in copies:
        copy.wait_send()


def body(queries, passages, clusters, lengths, feedback, ranks, cand_local, cand_count):
    grid = (SIZE["x"], SIZE["y"], SIZE["z"], CORES, QL, DIM)
    n_recv, n_pair = 320, 40
    vmem = pl.BlockSpec(memory_space=pltpu.VMEM)
    smem = pl.BlockSpec(memory_space=pltpu.SMEM)
    dma = pltpu.SemaphoreType.DMA
    rows = jnp.transpose(passages, (1, 0, 2)).reshape(PL * NP, DIM)
    lines = SIZE["x"] * SIZE["y"]
    width = SIZE["z"] * CORES
    out = pl.pallas_call(
        kernel,
        out_shape=jax.ShapeDtypeStruct((lines, width * CAP), F32),
        in_specs=[vmem, vmem, vmem, smem, vmem, vmem, vmem, vmem],
        out_specs=vmem,
        scratch_shapes=[
            pltpu.VMEM(grid, F32),
            pltpu.VMEM(grid, F32),
            pltpu.VMEM((QL, DIM), F32),
            pltpu.VMEM((NP * PL, 3 * DIM), BF16),
            pltpu.VMEM((NQ, FB * NQ), BF16),
            pltpu.VMEM((8, NQ), F32),
            pltpu.VMEM((lines, 1, DIM), F32),
            pltpu.VMEM((lines, 1, DIM), F32),
            pltpu.VMEM((width, CAP, DIM), F32),
            pltpu.VMEM((width, CAP, DIM), F32),
            dma((n_recv,)),
            dma((len(PARTS),)),
            dma((n_pair,)),
            dma((len(PARTS),)),
            dma((2,)),
            dma((lines - 1,)),
            dma((lines - 1,)),
            dma((width - 1,)),
            dma((width - 1,)),
        ],
        compiler_params=pltpu.CompilerParams(
            collective_id=0, has_side_effects=True, vmem_limit_bytes=56 << 20
        ),
        name="expand_and_score",
    )(queries, rows, clusters, lengths, feedback.T, ranks.T, cand_local.T, cand_count.T)
    return out.reshape(1, lines * width * CAP)


def solution(mesh):
    in_specs = (
        P(("query", "corpus"), None, None),
        P(("query", "corpus"), None, None),
        P(("query", "corpus"), None),
        P(("query", "corpus")),
        P(),
        P(),
        P(None, ("query", "corpus")),
        P(None, ("query", "corpus")),
    )
    out_specs = P(("query", "corpus"), None)
    return jax.shard_map(body, mesh=mesh, in_specs=in_specs, out_specs=out_specs, check_vma=False)
```

```python
import functools
import heapq
import math

import jax
import jax.numpy as jnp
from jax import lax
from jax.experimental import pallas as pl
from jax.experimental.pallas import tpu as pltpu
from jax.sharding import PartitionSpec as P

DIM = 128
QL = 32
PL = 180
NCENT = 24
EXP = 10
CAP = 2
FB = 3
NP = 4
NQ = 256
SIZE = {"x": 4, "y": 4, "z": 8}
CORES = 2
F32 = jnp.float32
BF16 = jnp.bfloat16
MESH = pl.DeviceIdType.MESH
WEIGHT = [0.5 * math.log((NCENT + 1.0) / (j + 1.0)) for j in range(EXP)]

PARTS = (
    ("q", 0, 8, "xyz"),
    ("q", 8, 8, "yzx"),
    ("q", 16, 16, "zxy"),
    ("i", 0, 8, "xyz"),
    ("i", 8, 16, "yzx"),
    ("i", 24, 8, "zxy"),
)
HOP_US = 1.8
LINK_GBS = 90.0
PAIR_US = 1.0
PAIR_GBS = 300.0
FINE = True
TASK_US = 0.25
EVERY = 2


def ring(n, anti):
    half = n // 2
    return {
        1: [-k for k in range(1, half + (anti == 1))],
        -1: [k for k in range(1, half + (anti == -1))],
    }


def displacements(n):
    return [0] + [s * k for k in range(1, n // 2) for s in (-1, 1)] + [n // 2]


def split3(v):
    hi = v.astype(BF16)
    rest = v - hi.astype(F32)
    mid = rest.astype(BF16)
    low = (rest - mid.astype(F32)).astype(BF16)
    return hi, mid, low


class Gather:
    def __init__(self, bufs, recv_sem, send_sem, pair_recv, pair_send):
        self.bufs = bufs
        self.recv_sem, self.send_sem = recv_sem, send_sem
        self.pair_recv, self.pair_send = pair_recv, pair_send
        corpus = lax.axis_index("corpus")
        zc = SIZE["z"] * CORES
        self.me = {
            "x": lax.axis_index("query"),
            "y": corpus // zc,
            "z": (corpus // CORES) % SIZE["z"],
            "c": corpus % CORES,
        }
        self.heap = []
        self.count = 0
        self.n_recv = 0
        self.n_pair = 0
        self.link = {}
        self.now = 0.0
        self.state = {}
        self.left = [0] * len(PARTS)

    def at(self, axis, d):
        if d == 0:
            return self.me[axis]
        n = SIZE[axis]
        return (self.me[axis] + (d % n)) & (n - 1)

    def device(self, **moved):
        pos = dict(self.me)
        pos.update(moved)
        return (pos["x"], (pos["y"] * SIZE["z"] + pos["z"]) * CORES + pos["c"])

    def region(self, part, sel, core):
        wave, row, rows, _ = PARTS[part]
        idx = []
        for axis in "xyz":
            d = sel[axis]
            idx.append(slice(None) if d is None else self.at(axis, d))
        return self.bufs[wave].at[idx[0], idx[1], idx[2], core, pl.ds(row, rows), :]

    def blocks(self, sel):
        return math.prod(SIZE[a] for a in "xyz" if sel[a] is None)

    def push(self, when, item):
        self.count += 1
        heapq.heappush(self.heap, (when, self.count, item))

    def send(self, part, stage, way, sel):
        axis = PARTS[part][3][stage]
        index = self.n_recv
        self.n_recv += 1
        ref = self.region(part, sel, self.me["c"])
        copy = pltpu.make_async_remote_copy(
            src_ref=ref,
            dst_ref=ref,
            send_sem=self.send_sem.at[part],
            recv_sem=self.recv_sem.at[index],
            device_id=self.device(**{axis: self.at(axis, way)}),
            device_id_type=MESH,
        )
        copy.start()
        bytes_ = self.blocks(sel) * PARTS[part][2] * DIM * 4
        key = (axis, way)
        begin = max(self.link.get(key, 0.0), self.now)
        self.link[key] = begin + 2 * bytes_ / (LINK_GBS * 1e3)
        self.now += 0.03
        got = dict(sel)
        got[axis] = sel[axis] - way
        self.push(self.link[key] + HOP_US, ("recv", part, stage, way, got, index))

    def pair(self, part, sel):
        index = self.n_pair
        self.n_pair += 1
        core = self.me["c"]
        ref = self.region(part, sel, core)
        copy = pltpu.make_async_remote_copy(
            src_ref=ref,
            dst_ref=ref,
            send_sem=self.pair_send.at[part],
            recv_sem=self.pair_recv.at[index],
            device_id=self.device(c=1 - core),
            device_id_type=MESH,
        )
        copy.start()
        bytes_ = self.blocks(sel) * PARTS[part][2] * DIM * 4
        begin = max(self.link.get("pair", 0.0), self.now)
        self.link["pair"] = begin + bytes_ / (PAIR_GBS * 1e3)
        self.now += 0.03
        self.push(self.link["pair"] + PAIR_US, ("pair", part, dict(sel), index))

    def ways(self, n, key, way, d):
        half = n // 2
        step = abs(d) + 1
        return step < half or (step == half and key == way)

    def start_stage(self, part, stage, sub, sel):
        n = SIZE[PARTS[part][3][stage]]
        anti = 1 if (sub + part) % 2 == 0 else -1
        for way in (1, -1):
            if self.ways(n, anti, way, 0):
                self.send(part, stage, way, sel)

    def begin(self, wave):
        for part, spec in enumerate(PARTS):
            if spec[0] != wave:
                continue
            a1, a2, a3 = spec[3]
            self.state[part] = {
                "line": set(), "plane": set(), "far": {}, "sub": {},
            }
            own = {"x": 0, "y": 0, "z": 0}
            self.start_stage(part, 0, 0, own)
        for part, spec in enumerate(PARTS):
            if spec[0] == wave:
                self.have1(part, 0)

    def have1(self, part, d1):
        a1, a2, a3 = PARTS[part][3]
        st = self.state[part]
        st["line"].add(d1)
        if FINE:
            sel = {a1: d1, a2: 0, a3: 0}
            sub = displacements(SIZE[a1]).index(d1)
            self.start_stage(part, 1, sub, sel)
        elif len(st["line"]) == SIZE[a1]:
            self.start_stage(part, 1, 0, {a1: None, a2: 0, a3: 0})
        if len(st["line"]) == SIZE[a1]:
            self.have2(part, 0)

    def got2(self, part, d2, sel):
        a1 = PARTS[part][3][0]
        st = self.state[part]
        if sel[a1] is None:
            self.have2(part, d2)
            return
        seen = st["sub"].setdefault(d2, set())
        seen.add(sel[a1])
        if len(seen) == SIZE[a1]:
            self.have2(part, d2)

    def have2(self, part, d2):
        a1, a2, a3 = PARTS[part][3]
        st = self.state[part]
        st["plane"].add(d2)
        sub = displacements(SIZE[a2]).index(d2)
        self.start_stage(part, 2, sub, {a1: None, a2: d2, a3: 0})
        if len(st["plane"]) == SIZE[a2]:
            self.pair(part, {a1: None, a2: None, a3: 0})

    def got3(self, part, d3, sel):
        a1, a2, a3 = PARTS[part][3]
        seen = self.state[part]["far"].setdefault(d3, set())
        seen.add(sel[a2])
        if len(seen) == SIZE[a2]:
            self.pair(part, {a1: None, a2: None, a3: d3})

    def canon(self, axis, d):
        n = SIZE[axis]
        return n // 2 if d is not None and abs(d) == n // 2 else d

    def handle(self, item):
        if item[0] == "pair":
            _, part, sel, index = item
            ref = self.region(part, sel, 1 - self.me["c"])
            pltpu.make_async_copy(ref, ref, self.pair_recv.at[index]).wait()
            return part
        _, part, stage, way, sel, index = item
        ref = self.region(part, sel, self.me["c"])
        pltpu.make_async_copy(ref, ref, self.recv_sem.at[index]).wait()
        order = PARTS[part][3]
        axis = order[stage]
        n = SIZE[axis]
        d = sel[axis]
        if stage == 0:
            sub = 0
        else:
            prev = order[stage - 1]
            sub = 0 if sel[prev] is None else displacements(SIZE[prev]).index(self.canon(prev, sel[prev]))
        anti = 1 if (sub + part) % 2 == 0 else -1
        if self.ways(n, anti, way, d):
            self.send(part, stage, way, sel)
        sel = dict(sel)
        sel[axis] = self.canon(axis, d)
        if stage == 0:
            self.have1(part, sel[axis])
        elif stage == 1:
            self.got2(part, sel[axis], sel)
        else:
            self.got3(part, sel[axis], sel)
        return None

    def step(self):
        when, _, item = heapq.heappop(self.heap)
        self.now = max(self.now, when)
        part = self.handle(item)
        self.now += 0.01
        if part is not None:
            self.left[part] += 1

    def advance(self, until):
        while self.heap and self.heap[0][0] <= until:
            self.step()
        self.now = max(self.now, until)

    def complete(self, part):
        return self.left[part] == SIZE[PARTS[part][3][2]]

    def run(self, tasks, every):
        tasks = list(tasks)
        count = 0
        while self.heap:
            self.step()
            count += 1
            ready = [t for t in tasks if self.complete(t[0])]
            if ready and count >= every:
                count = 0
                tasks.remove(ready[0])
                ready[0][1]()
                self.now += TASK_US
        for task in tasks:
            task[1]()
        assert all(self.complete(p) for p in range(len(PARTS)))

    def drain(self):
        for part, (wave, row, rows, _) in enumerate(PARTS):
            flat = self.bufs[wave].reshape(NQ, QL, DIM)
            ref = flat.at[pl.ds(0, NQ // 2 - 1), pl.ds(row, rows), :]
            pltpu.make_async_copy(ref, ref, self.send_sem.at[part]).wait()
            ref = flat.at[pl.ds(0, NQ // 2), pl.ds(row, rows), :]
            pltpu.make_async_copy(ref, ref, self.pair_send.at[part]).wait()


def iota(shape, axis):
    return lax.broadcasted_iota(jnp.int32, shape, axis)


def kernel(
    queries, rows_ref, clusters, lengths, feedback, ranks, cand, count, out,
    qbuf, ibuf, stage, p3, sel_ref, acc_ref,
    w_ref, r1_ref, m_ref, r2_ref,
    recv_sem, send_sem, pair_recv, pair_send, own_sem, a_send, a_recv, b_send, b_recv,
):
    gather = Gather({"q": qbuf, "i": ibuf}, recv_sem, send_sem, pair_recv, pair_send)
    me = gather.me
    home = lambda ref: ref.at[me["x"], me["y"], me["z"], me["c"]]

    own_q = pltpu.make_async_copy(queries.at[0], home(qbuf), own_sem.at[0])
    own_q.start()
    barrier = pltpu.get_barrier_semaphore()
    peers = [gather.device(**{a: gather.at(a, w)}) for a in "xyz" for w in (1, -1)]
    peers.append(gather.device(c=1 - me["c"]))
    for peer in peers:
        pl.semaphore_signal(barrier, inc=1, device_id=peer, device_id_type=MESH)
    pl.semaphore_wait(barrier, len(peers))
    own_q.wait()
    gather.begin("q")

    position = me["x"] * (NQ // 4) + (me["y"] * SIZE["z"] + me["z"]) * CORES + me["c"]
    fb = feedback[...]
    dev_row = (fb // NP).astype(F32)
    dev_col = jnp.transpose(jnp.concatenate([dev_row, jnp.zeros((8 - FB, NQ), F32)], axis=0))
    before = iota((NQ, NQ), 0) < iota((NQ, NQ), 1)
    turns = []
    for f in range(FB):
        total = jnp.zeros((NQ, NQ), F32)
        for g in range(FB):
            same = dev_col[:, g:g + 1] == dev_row[f:f + 1, :]
            if g == f:
                same = same & before
            if g <= f:
                total = total + jnp.where(same, 1.0, 0.0)
        turns.append(jnp.sum(total, axis=0, keepdims=True))
    turn_row = jnp.concatenate(turns, axis=0)

    gather.advance(2.0)

    rank_f = ranks[...].astype(F32)
    mine = dev_row == position.astype(F32)
    local_f = (fb % NP).astype(F32)
    columns, owners = [], []
    for i in range(FB):
        pick = jnp.where(mine & (turn_row == float(i)), 1.0, 0.0)
        owners.append(jnp.sum(jnp.sum(pick * local_f, axis=0, keepdims=True), axis=1, keepdims=True))
        who = jnp.sum(pick, axis=0, keepdims=True)
        columns.append(jnp.sum(rank_f * who, axis=1, keepdims=True))
    lane = iota((NCENT, QL), 1)
    turn = jnp.where(lane < EXP, 0, jnp.where(lane < 2 * EXP, 1, 2))
    place = (lane - turn * EXP).astype(F32)
    rank_of = jnp.where(turn == 0, columns[0], jnp.where(turn == 1, columns[1], columns[2]))
    owner_of = jnp.where(turn == 0, owners[0], jnp.where(turn == 1, owners[1], owners[2]))
    wanted = (rank_of == place) & (lane < FB * EXP)
    gather.advance(3.5)
    token = iota((NCENT, PL), 1)
    centre = iota((NCENT, PL), 0)
    asks, sums = [], []
    for p in range(NP):
        member = (clusters[p:p + 1, :] == centre) & (token < lengths[p])
        member = jnp.where(member, 1.0, 0.0).astype(BF16)
        tile = jnp.concatenate(split3(rows_ref[pl.ds(p, PL, stride=NP), :]), axis=1)
        part = jnp.dot(member, tile, preferred_element_type=F32)
        sums.append(part[:, :DIM] + part[:, DIM:2 * DIM] + part[:, 2 * DIM:])
        gather.advance(4.2 + 0.7 * p)
        asks.append(jnp.where(wanted & (owner_of == float(p)), 1.0, 0.0))
    asks = jnp.transpose(jnp.concatenate(asks, axis=0)).astype(BF16)
    tile = jnp.concatenate(split3(jnp.concatenate(sums, axis=0)), axis=1)
    items = jnp.dot(asks, tile, preferred_element_type=F32)
    stage[...] = items[:, :DIM] + items[:, DIM:2 * DIM] + items[:, 2 * DIM:]

    own_i = pltpu.make_async_copy(stage, home(ibuf), own_sem.at[1])
    own_i.start()

    turn_col = jnp.transpose(jnp.concatenate([turn_row, jnp.zeros((8 - FB, NQ), F32)], axis=0))
    device = iota((NQ, NQ), 1).astype(F32)
    for i in range(FB):
        total = jnp.zeros((NQ, NQ), F32)
        for f in range(FB):
            hit = (dev_col[:, f:f + 1] == device) & (turn_col[:, f:f + 1] == float(i))
            total = total + jnp.where(hit, 1.0, 0.0)
        sel_ref[:, i * NQ:(i + 1) * NQ] = total.astype(BF16)
        if i == 0:
            own_i.wait()
            gather.advance(8.0)
            gather.begin("i")
        gather.advance(8.0 + 0.5 * i)

    live = rows_ref[...]
    row = iota((NP * PL, 1), 0)
    slot = row % NP
    length = jnp.where(slot == 0, lengths[0], jnp.where(slot == 1, lengths[1], jnp.where(slot == 2, lengths[2], lengths[3])))
    head = rows_ref[0:NP, :]
    head = jnp.concatenate([head, head] * (PL // 2), axis=0)
    live = jnp.where(row // NP < length, live, head)
    hi = live.astype(BF16)
    low = (live - hi.astype(F32)).astype(BF16)
    p3[:, 0:DIM] = hi
    p3[:, DIM:] = low
    acc_ref[...] = jnp.zeros_like(acc_ref)

    gather.advance(11.0)

    def add_rows(tile):
        hi = tile.astype(BF16)
        rhs = jnp.concatenate([hi, hi], axis=1)
        similar = lax.dot_general(p3[...], rhs, (((1,), (1,)), ((), ())), preferred_element_type=F32)
        best = jnp.max(similar.reshape(NP * PL // 8, 8, NQ), axis=0)
        acc_ref[...] += jnp.maximum(best, pltpu.roll(best, 4, 0))

    qflat = qbuf.reshape(NQ * QL, DIM)
    iflat = ibuf.reshape(NQ * QL, DIM)

    def score_queries(first, n):
        @pl.loop(first, first + n)
        def _(t):
            add_rows(qflat[pl.ds(t, NQ, stride=QL), :])

    tasks = []
    for part, (wave, row, rows, _) in enumerate(PARTS):
        if wave == "q":
            tasks += [(part, functools.partial(score_queries, t, 1)) for t in range(row, row + rows)]
    gather.run(tasks, EVERY)

    @pl.loop(0, EXP)
    def _(j):
        pieces = [iflat[pl.ds(j + i * EXP, NQ, stride=QL), :] for i in range(FB)]
        tile = jnp.concatenate(pieces, axis=0)
        hi = tile.astype(BF16)
        low = (tile - hi.astype(F32)).astype(BF16)
        both = jnp.dot(sel_ref[...], jnp.concatenate([hi, low], axis=1), preferred_element_type=F32)
        total = both[:, :DIM] + both[:, DIM:]
        weight = jnp.float32(WEIGHT[EXP - 1])
        for k in range(EXP - 1):
            weight = jnp.where(j == k, jnp.float32(WEIGHT[k]), weight)
        scale = lax.rsqrt(jnp.mean(total * total, axis=1, keepdims=True) + 1e-05)
        add_rows(total * scale * weight)

    gather.drain()

    lines = SIZE["x"] * SIZE["y"]
    width = SIZE["z"] * CORES
    picked = cand[...]
    live_slots = count[...]
    w = jnp.zeros((lines, DIM), F32)
    own_row = iota((lines, NQ), 1) // width == iota((lines, NQ), 0)
    for s in range(CAP):
        value = jnp.zeros((1, NQ), F32)
        for p in range(NP):
            value = value + jnp.where(picked[s:s + 1, :] == p, acc_ref[p:p + 1, :], 0.0)
        value = jnp.where(live_slots > s, value * (1.0 / QL), 0.0)
        spread = jnp.where(own_row, value, 0.0)
        put = iota((NQ, DIM), 0) % width * CAP + s == iota((NQ, DIM), 1)
        put = jnp.where(put, 1.0, 0.0).astype(BF16)
        for term in split3(spread):
            w = w + jnp.dot(term, put, preferred_element_type=F32)
    for r in range(lines):
        w_ref[r] = w[r:r + 1, :]

    exchange(gather, w_ref, r1_ref, a_send, a_recv, "xy")
    r1 = jnp.concatenate([r1_ref[r] for r in range(lines)], axis=0)
    turned = jnp.transpose(r1)
    for r in range(width):
        m_ref[r, :, 0:lines] = turned[r * CAP:(r + 1) * CAP, :]
    exchange(gather, m_ref, r2_ref, b_send, b_recv, "zc")
    r2 = jnp.concatenate([r2_ref[r] for r in range(width)], axis=0)
    out[...] = jnp.transpose(r2)[0:lines, :]


def exchange(gather, src, dst, send_sem, recv_sem, axes):
    me = gather.me
    sizes = {"x": SIZE["x"], "y": SIZE["y"], "z": SIZE["z"], "c": CORES}
    a, b = axes
    mine = me[a] * sizes[b] + me[b]
    steps = []
    for da in range(sizes[a]):
        for db in range(sizes[b]):
            if da or db:
                far = min(da, sizes[a] - da) + (min(db, sizes[b] - db) if b != "c" else 0.3 * db)
                steps.append((-far, da, db))
    steps.sort()
    copies = []
    for k, (_, da, db) in enumerate(steps):
        ta = (me[a] + da) & (sizes[a] - 1)
        tb = (me[b] + db) & (sizes[b] - 1)
        copy = pltpu.make_async_remote_copy(
            src_ref=src.at[ta * sizes[b] + tb],
            dst_ref=dst.at[mine],
            send_sem=send_sem.at[k],
            recv_sem=recv_sem.at[k],
            device_id=gather.device(**{a: ta, b: tb}),
            device_id_type=MESH,
        )
        copy.start()
        copies.append((copy, da, db))
    dst[mine] = src[mine]
    for k, (copy, da, db) in enumerate(copies):
        fa = (me[a] - da) & (sizes[a] - 1)
        fb = (me[b] - db) & (sizes[b] - 1)
        ref = dst.at[fa * sizes[b] + fb]
        pltpu.make_async_copy(ref, ref, recv_sem.at[k]).wait()
    for copy, _, _ in copies:
        copy.wait_send()


def body(queries, passages, clusters, lengths, feedback, ranks, cand_local, cand_count):
    grid = (SIZE["x"], SIZE["y"], SIZE["z"], CORES, QL, DIM)
    n_recv, n_pair = 320, 40
    vmem = pl.BlockSpec(memory_space=pltpu.VMEM)
    smem = pl.BlockSpec(memory_space=pltpu.SMEM)
    dma = pltpu.SemaphoreType.DMA
    rows = jnp.transpose(passages, (1, 0, 2)).reshape(PL * NP, DIM)
    lines = SIZE["x"] * SIZE["y"]
    width = SIZE["z"] * CORES
    out = pl.pallas_call(
        kernel,
        out_shape=jax.ShapeDtypeStruct((lines, width * CAP), F32),
        in_specs=[vmem, vmem, vmem, smem, vmem, vmem, vmem, vmem],
        out_specs=vmem,
        scratch_shapes=[
            pltpu.VMEM(grid, F32),
            pltpu.VMEM(grid, F32),
            pltpu.VMEM((QL, DIM), F32),
            pltpu.VMEM((NP * PL, 2 * DIM), BF16),
            pltpu.VMEM((NQ, FB * NQ), BF16),
            pltpu.VMEM((8, NQ), F32),
            pltpu.VMEM((lines, 1, DIM), F32),
            pltpu.VMEM((lines, 1, DIM), F32),
            pltpu.VMEM((width, CAP, DIM), F32),
            pltpu.VMEM((width, CAP, DIM), F32),
            dma((n_recv,)),
            dma((len(PARTS),)),
            dma((n_pair,)),
            dma((len(PARTS),)),
            dma((2,)),
            dma((lines - 1,)),
            dma((lines - 1,)),
            dma((width - 1,)),
            dma((width - 1,)),
        ],
        compiler_params=pltpu.CompilerParams(
            collective_id=0, has_side_effects=True, vmem_limit_bytes=56 << 20
        ),
        name="expand_and_score",
    )(queries, rows, clusters, lengths, feedback.T, ranks.T, cand_local.T, cand_count.T)
    return out.reshape(1, lines * width * CAP)


def solution(mesh):
    in_specs = (
        P(("query", "corpus"), None, None),
        P(("query", "corpus"), None, None),
        P(("query", "corpus"), None),
        P(("query", "corpus")),
        P(),
        P(),
        P(None, ("query", "corpus")),
        P(None, ("query", "corpus")),
    )
    out_specs = P(("query", "corpus"), None)
    return jax.shard_map(body, mesh=mesh, in_specs=in_specs, out_specs=out_specs, check_vma=False)
```
